32 devices in a mesh: ctx: 4 (over z), pipe: 2 (over x), tp: 4 (over y, core).
Axes of the slice: x: 2, y: 2, z: 4, core: 2. Of those that a mesh axis runs over, the one named last changes fastest.
Arguments:
- upstream: bfloat16 [2, 512, 2688], P('pipe', 'ctx', 'tp'), may hold values from -6 to 6
- saved_input: bfloat16 [2, 512, 2688], P('pipe', 'ctx', 'tp'), may hold values from -0.59765625 to 0.59765625
- inv_rms: float32 [2, 512], P('pipe', 'ctx'), may hold values from 2 to 20
- norm_gain: float32 [2, 2688], P('pipe', 'tp'), may hold values from 0.1 to 1.9
- query_proj: bfloat16 [2, 512, 2048], P('pipe', 'ctx', 'tp'), may hold values from -14 to 14
- key_proj: bfloat16 [2, 512, 1024], P('pipe', 'ctx', 'tp'), may hold values from -5.2 to 5.2
- stored_value_rows: bfloat16 [2, 512, 1024], P('pipe', 'ctx', 'tp'), may hold values from -6 to 6
- attn_out: bfloat16 [2, 512, 2048], P('pipe', 'ctx', 'tp'), may hold values from -6 to 6
- w_query: bfloat16 [2, 2688, 2048], P('pipe', None, 'tp'), may hold values from -0.125 to 0.125
- key_projection_weight: bfloat16 [2, 2688, 1024], P('pipe', None, 'tp'), may hold values from -0.125 to 0.125
- value_projection_weight: bfloat16 [2, 2688, 1024], P('pipe', None, 'tp'), may hold values from -0.125 to 0.125
- w_out: bfloat16 [2, 2048, 2688], P('pipe', 'tp'), may hold values from -0.125 to 0.125
- seq_lengths: int32 [2], P('pipe'), may hold values from 256 to 512, as said below
Outputs:
- next_grad: bfloat16 [2, 512, 2688], P('pipe', 'ctx', 'tp')
The draws below stay inside these ranges and needn't reach their ends.
Inputs may be any that keep to these rules, and one draw needn't show every extreme that they name: `seq_lengths`: valid tokens come first in each sequence; at least one section's sequence has all 512 tokens valid.
All inputs are finite; a program needn't handle non-finite values.
Results may differ from the reference program's by a relative error of at most 0.0062.
Values may be sent and summed in bfloat16 or wider, within the bound.
A program may use at most 64 MiB of HBM per device.

```python
import math
import jax
import jax.numpy as jnp
from jax import lax

MODEL_WIDTH = 2688
QUERY_HEADS = 16
KEY_VALUE_HEADS = 8
HEAD_SIZE = 128
WINDOW = 1024
QUERY_SCALAR = 168
TOK_DEV = 128
RELAY_SECTIONS = 2
SEQUENCE_TOKENS = 512


def joint_projections(key):
    query_group_width = QUERY_HEADS // KEY_VALUE_HEADS
    key_start_row = jax.random.fold_in(key, 101)
    query_start_row = jax.random.fold_in(key, 202)
    key_entries = jnp.clip(jax.random.normal(key_start_row, (RELAY_SECTIONS, SEQUENCE_TOKENS, KEY_VALUE_HEADS, HEAD_SIZE), jnp.float32), -4.0, 4.0)
    query_entries = jnp.clip(jax.random.normal(query_start_row, (RELAY_SECTIONS, SEQUENCE_TOKENS, KEY_VALUE_HEADS, query_group_width, HEAD_SIZE), jnp.float32), -4.0, 4.0)
    return (query_entries.reshape(RELAY_SECTIONS, SEQUENCE_TOKENS, QUERY_HEADS * HEAD_SIZE), key_entries.reshape(RELAY_SECTIONS, SEQUENCE_TOKENS, KEY_VALUE_HEADS * HEAD_SIZE))


def draw_query_proj(key, part):
    return joint_projections(key)[0].astype(jnp.bfloat16)


def draw_key_proj(key, part):
    return joint_projections(key)[1].astype(jnp.bfloat16)


def draw_seq_lengths(key, part):
    first_key = jax.random.fold_in(key, 505)
    second_key = jax.random.fold_in(key, 606)
    lengths_drawn = jax.random.randint(first_key, (RELAY_SECTIONS,), SEQUENCE_TOKENS // 2, SEQUENCE_TOKENS + 1)
    chosen = jax.random.randint(second_key, (), 0, RELAY_SECTIONS)
    return jnp.where(jnp.arange(RELAY_SECTIONS) == chosen, SEQUENCE_TOKENS, lengths_drawn).astype(jnp.int32)


def block_scale(key, extent, split, least, top_value):
    gain, own = 1.0, jax.random.fold_in(key, 6)
    for dim, shards_of in split:
        heights = jnp.exp(jax.random.uniform(jax.random.fold_in(own, dim), (shards_of,), jnp.float32, least / len(split), top_value / len(split)))
        gain = gain * jnp.repeat(heights, extent[dim] // shards_of).reshape([-1 if axis == dim else 1 for axis in range(len(extent))])
    return gain


def normal_values(stream_key, shape, deviation, limit, split=(), kind=jnp.bfloat16):
    drawn = deviation * jax.random.normal(stream_key, shape, jnp.float32)
    if split:
        drawn = drawn * block_scale(stream_key, shape, split, -0.22, 0.18)
    return jnp.clip(drawn, -limit, limit).astype(kind)


def setup_inputs(seed: int = 0) -> dict:
    seeds = jax.random.split(jax.random.key(seed), 14)
    return {
        "upstream": normal_values(seeds[0], (RELAY_SECTIONS, SEQUENCE_TOKENS, MODEL_WIDTH), 1.0, 6.0, ((0, 2), (1, 4), (2, 4))),
        "saved_input": normal_values(seeds[1], (RELAY_SECTIONS, SEQUENCE_TOKENS, MODEL_WIDTH), 0.1, 0.59765625, ((0, 2), (1, 4), (2, 4))),
        "inv_rms": jnp.clip(jnp.exp(math.log(20.0) - 2.3025851 * jax.random.uniform(seeds[2], (RELAY_SECTIONS, SEQUENCE_TOKENS), jnp.float32) ** block_scale(seeds[2], (RELAY_SECTIONS, SEQUENCE_TOKENS), ((0, 2), (1, 4)), -0.2, 0.2)), 2.0, 20.0),
        "norm_gain": jnp.clip(1.0 + 0.18 * jax.random.normal(seeds[3], (RELAY_SECTIONS, MODEL_WIDTH), jnp.float32), 0.1, 1.9),
        "query_proj": draw_query_proj(jax.random.fold_in(seeds[13], 71), 0),
        "key_proj": draw_key_proj(jax.random.fold_in(seeds[13], 71), 0),
        "stored_value_rows": normal_values(seeds[6], (RELAY_SECTIONS, SEQUENCE_TOKENS, KEY_VALUE_HEADS * HEAD_SIZE), 1.0, 6.0, ((0, 2), (1, 4), (2, 4))),
        "attn_out": normal_values(seeds[7], (RELAY_SECTIONS, SEQUENCE_TOKENS, QUERY_HEADS * HEAD_SIZE), 1.0, 6.0, ((0, 2), (1, 4), (2, 4))),
        "w_query": normal_values(seeds[8], (RELAY_SECTIONS, MODEL_WIDTH, QUERY_HEADS * HEAD_SIZE), MODEL_WIDTH ** -0.5, 0.125, ((0, 2), (2, 4))),
        "key_projection_weight": normal_values(seeds[9], (RELAY_SECTIONS, MODEL_WIDTH, KEY_VALUE_HEADS * HEAD_SIZE), MODEL_WIDTH ** -0.5, 0.125, ((0, 2), (2, 4))),
        "value_projection_weight": normal_values(seeds[10], (RELAY_SECTIONS, MODEL_WIDTH, KEY_VALUE_HEADS * HEAD_SIZE), MODEL_WIDTH ** -0.5, 0.125, ((0, 2), (2, 4))),
        "w_out": normal_values(seeds[11], (RELAY_SECTIONS, QUERY_HEADS * HEAD_SIZE, MODEL_WIDTH), (QUERY_HEADS * HEAD_SIZE) ** -0.5, 0.125, ((0, 2), (1, 4))),
        "seq_lengths": draw_seq_lengths(jax.random.fold_in(seeds[13], 71), 0),
    }


NEG_FILL = -1.0e30
CONTRACT_LAST = (((1,), (1,)), ((), ()))


def window_mask(pos_query, pos_key, length):
    later = pos_query[:, None] - pos_key[None, :]
    inside = (later >= 0) & (later < WINDOW) & (pos_key[None, :] >= 0)
    return inside & (pos_key[None, :] < length) & (pos_query[:, None] < length)


def block_grads(query_block_rows, output_grad_block, output_block, key_block_rows, value_block_rows, pos_query, pos_key, length):
    score_scale = QUERY_SCALAR ** -0.5
    query_group_width = QUERY_HEADS // KEY_VALUE_HEADS
    block_row_count = query_block_rows.shape[0]
    key_total_count = key_block_rows.shape[0]
    query_head_rows = query_block_rows.astype(jnp.float32).reshape(block_row_count, KEY_VALUE_HEADS, query_group_width, HEAD_SIZE)
    output_grad_heads = output_grad_block.astype(jnp.float32).reshape(block_row_count, KEY_VALUE_HEADS, query_group_width, HEAD_SIZE)
    output_heads = output_block.astype(jnp.float32).reshape(block_row_count, KEY_VALUE_HEADS, query_group_width, HEAD_SIZE)
    key_head_rows = key_block_rows.astype(jnp.float32).reshape(key_total_count, KEY_VALUE_HEADS, HEAD_SIZE)
    value_head_rows = value_block_rows.astype(jnp.float32).reshape(key_total_count, KEY_VALUE_HEADS, HEAD_SIZE)
    allowed = window_mask(pos_query, pos_key, length)
    live_rows = pos_query < length
    scores = jnp.einsum('tgrd,kgd->grtk', query_head_rows, key_head_rows) * score_scale
    scores = jnp.where(allowed, scores, NEG_FILL)
    top_score = jnp.max(scores, axis=-1, keepdims=True)
    raised = jnp.where(allowed, jnp.exp(scores - top_score), 0.0)
    row_total = jnp.sum(raised, axis=-1, keepdims=True)
    weights = raised / jnp.where(live_rows[:, None], row_total, 1.0)
    output_dot_grad = jnp.einsum('uhap,uhap->hau', output_grad_heads, output_heads)
    dprob = jnp.einsum('tgrd,kgd->grtk', output_grad_heads, value_head_rows)
    dscore = (weights * (dprob - output_dot_grad[..., None])).astype(jnp.bfloat16)
    weights_low = weights.astype(jnp.bfloat16)
    dscore_wide = lax.optimization_barrier(dscore).astype(jnp.float32)
    weights_wide = lax.optimization_barrier(weights_low).astype(jnp.float32)
    query_gradient = (jnp.einsum('grtk,kgd->tgrd', dscore_wide, key_head_rows) * score_scale).astype(jnp.bfloat16)
    key_gradient = jnp.einsum('grtk,tgrd->kgd', dscore_wide, query_head_rows) * score_scale
    value_gradient = jnp.einsum('grtk,tgrd->kgd', weights_wide, output_grad_heads)
    return (query_gradient.reshape(block_row_count, QUERY_HEADS * HEAD_SIZE), key_gradient.reshape(key_total_count, KEY_VALUE_HEADS * HEAD_SIZE),
            value_gradient.reshape(key_total_count, KEY_VALUE_HEADS * HEAD_SIZE))


def section_grads(grad_in, inputs, inv_row, gain_row, queries, key_row_span, value_row_span, out_rows,
                weight_query, weight_key, weight_value, weight_out, length):
    reach = (WINDOW - 2 + TOK_DEV) // TOK_DEV
    border_rows = reach * TOK_DEV
    grad_out = lax.dot_general(grad_in, weight_out, CONTRACT_LAST,
                               preferred_element_type=jnp.float32).astype(jnp.bfloat16)
    key_with_padding = jnp.concatenate([jnp.zeros((border_rows, KEY_VALUE_HEADS * HEAD_SIZE), key_row_span.dtype), key_row_span], axis=0)
    value_with_padding = jnp.concatenate([jnp.zeros((border_rows, KEY_VALUE_HEADS * HEAD_SIZE), value_row_span.dtype), value_row_span], axis=0)

    def advance(carry, block_index):
        key_acc, value_acc = carry
        anchor = (block_index * TOK_DEV).astype(jnp.int32)
        pos_query = anchor + lax.iota(jnp.int32, TOK_DEV)
        pos_key = anchor - border_rows + lax.iota(jnp.int32, border_rows + TOK_DEV)
        query_gradient, key_gradient, value_gradient = block_grads(
            lax.dynamic_slice_in_dim(queries, anchor, TOK_DEV, 0),
            lax.dynamic_slice_in_dim(grad_out, anchor, TOK_DEV, 0),
            lax.dynamic_slice_in_dim(out_rows, anchor, TOK_DEV, 0),
            lax.dynamic_slice_in_dim(key_with_padding, anchor, border_rows + TOK_DEV, 0),
            lax.dynamic_slice_in_dim(value_with_padding, anchor, border_rows + TOK_DEV, 0),
            pos_query, pos_key, length)
        key_acc = lax.dynamic_update_slice_in_dim(
            key_acc, lax.dynamic_slice_in_dim(key_acc, anchor, border_rows + TOK_DEV, 0) + key_gradient, anchor, 0)
        value_acc = lax.dynamic_update_slice_in_dim(
            value_acc, lax.dynamic_slice_in_dim(value_acc, anchor, border_rows + TOK_DEV, 0) + value_gradient, anchor, 0)
        return (key_acc, value_acc), query_gradient

    initial_totals = jnp.zeros((border_rows + SEQUENCE_TOKENS, KEY_VALUE_HEADS * HEAD_SIZE), jnp.float32)
    (key_acc, value_acc), query_blocks = lax.scan(
        advance, (initial_totals, initial_totals), jnp.arange(SEQUENCE_TOKENS // TOK_DEV, dtype=jnp.int32))
    query_gradient = query_blocks.reshape(SEQUENCE_TOKENS, QUERY_HEADS * HEAD_SIZE)
    key_gradient = key_acc[border_rows:].astype(jnp.bfloat16)
    value_gradient = value_acc[border_rows:].astype(jnp.bfloat16)
    normed_grad = (lax.dot_general(query_gradient, weight_query, CONTRACT_LAST, preferred_element_type=jnp.float32)
                   + lax.dot_general(key_gradient, weight_key, CONTRACT_LAST, preferred_element_type=jnp.float32)
                   + lax.dot_general(value_gradient, weight_value, CONTRACT_LAST, preferred_element_type=jnp.float32))
    coupling = (jnp.sum(query_gradient.astype(jnp.float32) * queries.astype(jnp.float32), axis=1)
                + jnp.sum(key_gradient.astype(jnp.float32) * key_row_span.astype(jnp.float32), axis=1)
                + jnp.sum(value_gradient.astype(jnp.float32) * value_row_span.astype(jnp.float32), axis=1))
    scale_rows = inv_row[:, None]
    result = grad_in.astype(jnp.float32) + scale_rows * (
        gain_row[None, :] * normed_grad - inputs.astype(jnp.float32) * scale_rows * coupling[:, None] / MODEL_WIDTH)
    return result.astype(jnp.bfloat16)


def reference(upstream, saved_input, inv_rms, norm_gain, query_proj, key_proj, stored_value_rows, attn_out,
              w_query, key_projection_weight, value_projection_weight, w_out, seq_lengths):
    results = []
    for section in range(RELAY_SECTIONS):
        results.append(section_grads(upstream[section], saved_input[section], inv_rms[section], norm_gain[section],
                                   query_proj[section], key_proj[section], stored_value_rows[section], attn_out[section],
                                   w_query[section], key_projection_weight[section], value_projection_weight[section], w_out[section],
                                   seq_lengths[section]))
    stacked = jnp.stack(results, axis=0)
    return jnp.roll(stacked, -1, axis=0)
```

```python
import functools

import jax
import jax.numpy as jnp
from jax import lax
from jax.experimental import pallas as pl
from jax.experimental.pallas import tpu as pltpu
from jax.sharding import PartitionSpec as P

QUERY_HEADS = 16
KEY_VALUE_HEADS = 8
HEAD_SIZE = 128
WINDOW = 1024
QUERY_SCALAR = 168
NEG_FILL = -1e30
ROW_CHUNKS = 4
NT = (((1,), (1,)), ((), ()))
NN = (((1,), (0,)), ((), ()))
TN = (((0,), (0,)), ((), ()))
BF = jnp.bfloat16
F32 = jnp.float32


def dot(a, b, dims):
    return lax.dot_general(a, b, dims, preferred_element_type=F32)


def kernel(
    ctx_n,
    pipe_n,
    reach,
    up_h,
    xin_h,
    inv_h,
    gain_h,
    q_h,
    k_h,
    v_h,
    ao_h,
    wq_h,
    wk_h,
    wv_h,
    wo_h,
    len_h,
    out_h,
    gath,
    xin,
    inv,
    gain,
    q,
    kb,
    vb,
    ao,
    wq,
    wk,
    wv,
    wo,
    slen,
    dout,
    dos,
    qs,
    s,
    part_k,
    part_v,
    snd_k,
    snd_v,
    rcv_k,
    rcv_v,
    dq,
    pacc,
    rs_a,
    rs_ar,
    rs_b,
    rs_br,
    rs_c,
    rs_cr,
    res,
    lsem,
    k_s,
    k_r,
    v_s,
    v_r,
    ag_s,
    ag_r,
    dk_s,
    dk_r,
    dv_s,
    dv_r,
    rs_s,
    rs_rv,
    x_s,
    x_r,
):
    i = lax.axis_index("ctx")
    p = lax.axis_index("pipe")
    t = lax.axis_index("tp")
    partner = t + 1 - 2 * (t % 2)
    cross = (t + 2) % 4
    diag = 3 - t
    rows = q.shape[0]
    width = xin.shape[1]
    kv_heads = kb.shape[2] // HEAD_SIZE
    group = q.shape[1] // kb.shape[2]
    stacked = group * rows
    scale = QUERY_SCALAR ** (-0.5)
    model_width = width * 4

    def local(src, dst, n):
        c = pltpu.make_async_copy(src, dst, lsem.at[n])
        c.start()
        return c

    def remote(src, dst, ss, rs, dev):
        return pltpu.make_async_remote_copy(
            src_ref=src,
            dst_ref=dst,
            send_sem=ss,
            recv_sem=rs,
            device_id=dev,
            device_id_type=pl.DeviceIdType.MESH,
        )

    c_k = local(k_h, kb.at[0], 0)
    c_q = local(q_h, q, 1)
    c_len = local(len_h, slen, 2)
    c_up = local(up_h, gath.at[t], 3)
    c_v = local(v_h, vb.at[0], 4)
    c_wo = local(wo_h, wo, 5)
    c_ao = local(ao_h, ao, 6)
    c_wq = local(wq_h, wq, 7)
    c_wk = local(wk_h, wk, 8)
    c_wv = local(wv_h, wv, 9)
    c_xin = local(xin_h, xin, 10)
    c_inv = local(inv_h, inv, 11)
    c_gain = local(gain_h, gain, 12)

    barrier = pltpu.get_barrier_semaphore()

    def greet(dev):
        pl.semaphore_signal(
            barrier, inc=1, device_id=dev, device_id_type=pl.DeviceIdType.MESH
        )

    has_up = i + 1 < ctx_n
    has_down = i > 0

    @pl.when(has_up)
    def _():
        greet({"ctx": i + 1})

    @pl.when(has_down)
    def _():
        greet({"ctx": i - 1})

    greet({"tp": partner})
    greet({"tp": cross})
    expect = 2
    prev = (p + pipe_n - 1) % pipe_n
    if pipe_n > 1:
        greet({"pipe": prev})
        expect += 1
    if pipe_n > 2:
        greet({"pipe": (p + 1) % pipe_n})
        expect += 1
    pl.semaphore_wait(
        barrier, expect + jnp.where(has_up, 1, 0) + jnp.where(has_down, 1, 0)
    )

    up_dev = {"ctx": i + 1}
    down_dev = {"ctx": i - 1}

    def k_copy(d):
        src = k_h if d == 0 else kb.at[d]
        return remote(src, kb.at[d + 1], k_s.at[d], k_r.at[d + 1], up_dev)

    def v_copy(d):
        src = v_h if d == 0 else vb.at[d]
        return remote(src, vb.at[d + 1], v_s.at[d], v_r.at[d + 1], up_dev)

    ag_cross = remote(up_h, gath.at[t], ag_s.at[0], ag_r.at[0], {"tp": cross})
    ag_part = remote(up_h, gath.at[t], ag_s.at[1], ag_r.at[1], {"tp": partner})
    ag_fwd = remote(
        gath.at[cross], gath.at[cross], ag_s.at[2], ag_r.at[2], {"tp": partner}
    )
    ag_cross.start()

    @pl.when(has_up)
    def _():
        k_copy(0).start()
        v_copy(0).start()

    ag_part.start()

    c_len.wait()
    length = slen[0]
    key_i = lax.broadcasted_iota(jnp.int32, (rows, stacked), 0)
    qry_i = lax.broadcasted_iota(jnp.int32, (rows, stacked), 1) % rows
    later0 = qry_i - key_i
    pos_q = i * rows + qry_i
    live = pos_q < length

    def scores(d):
        later = later0 + d * rows
        pos_k = pos_q - later
        ok = (later >= 0) & (later < WINDOW) & (pos_k < length) & live
        for g in range(kv_heads):
            cols = slice(g * HEAD_SIZE, (g + 1) * HEAD_SIZE)
            sc = dot(kb[d, :, cols], qs[g], NT) * scale
            s[d, g] = jnp.where(ok, sc, NEG_FILL)

    c_q.wait()
    for g in range(kv_heads):
        for r in range(group):
            h = g * group + r
            qs[g, r * rows : (r + 1) * rows, :] = q[:, h * HEAD_SIZE : (h + 1) * HEAD_SIZE]
    c_k.wait()
    scores(0)

    def take(d):
        @pl.when(i >= d)
        def _():
            k_copy(d - 1).wait_recv()
            if d < reach:

                @pl.when(has_up)
                def _():
                    k_copy(d).start()

            scores(d)
            v_copy(d - 1).wait_recv()
            if d < reach:

                @pl.when(has_up)
                def _():
                    v_copy(d).start()

    if reach >= 1:
        take(1)
    ag_cross.wait_recv()
    ag_fwd.start()
    for d in range(2, reach + 1):
        take(d)

    ag_part.wait_recv()
    ag_fwd.wait_recv()
    c_up.wait()
    c_wo.wait()
    whole = jnp.concatenate([gath[n] for n in range(4)], axis=1)
    dout[...] = dot(whole, wo[...], NT).astype(BF)
    c_ao.wait()
    deltas = []
    for g in range(kv_heads):
        prods = []
        for r in range(group):
            h = g * group + r
            cols = slice(h * HEAD_SIZE, (h + 1) * HEAD_SIZE)
            grad = dout[:, cols]
            dos[g, r * rows : (r + 1) * rows, :] = grad
            prod = grad.astype(F32) * ao[:, cols].astype(F32)
            prods.append(jnp.sum(prod.T, axis=0, keepdims=True))
        deltas.append(jnp.concatenate(prods, axis=1))

    for d in range(1, reach + 1):

        @pl.when(i < d)
        def _():
            s[d] = jnp.full(s.shape[1:], NEG_FILL, F32)

    tops, inv_totals = [], []
    for g in range(kv_heads):
        top = jnp.max(s[0, g], axis=0, keepdims=True)
        for d in range(1, reach + 1):
            top = jnp.maximum(top, jnp.max(s[d, g], axis=0, keepdims=True))
        total = jnp.zeros((1, stacked), F32)
        for d in range(reach + 1):
            val = s[d, g]
            e = jnp.where(val > 0.5 * NEG_FILL, jnp.exp(val - top), 0.0)
            s[d, g] = e
            total = total + jnp.sum(e, axis=0, keepdims=True)
        inv_totals.append(1.0 / jnp.where(live[:1], total, 1.0))

    c_v.wait()

    def dk_copy(d):
        return remote(snd_k.at[d], rcv_k.at[d - 1], dk_s.at[d], dk_r.at[d - 1], down_dev)

    def dv_copy(d):
        return remote(snd_v.at[d], rcv_v.at[d - 1], dv_s.at[d], dv_r.at[d - 1], down_dev)

    dq[...] = jnp.zeros_like(dq)

    def first_of_chain(d):
        return i + 1 >= ctx_n if d < reach else i >= d

    def block(d):
        probs = []
        for g in range(kv_heads):
            cols = slice(g * HEAD_SIZE, (g + 1) * HEAD_SIZE)
            prob = s[d, g] * inv_totals[g]
            probs.append(prob)
            part_v[d, :, cols] = dot(prob.astype(BF), dos[g], NN)
        if d > 0:

            @pl.when(first_of_chain(d))
            def _():
                snd_v[d] = part_v[d].astype(BF)
                dv_copy(d).start()

        for g in range(kv_heads):
            cols = slice(g * HEAD_SIZE, (g + 1) * HEAD_SIZE)
            dprob = dot(vb[d, :, cols], dos[g], NT)
            ds = (probs[g] * (dprob - deltas[g])).astype(BF)
            part_k[d, :, cols] = dot(ds, qs[g], NN)
            dq[g] += dot(ds, kb[d, :, cols], TN)
        if d > 0:

            @pl.when(first_of_chain(d))
            def _():
                snd_k[d] = part_k[d].astype(BF)
                dk_copy(d).start()

    for d in range(reach, 0, -1):
        pl.when(i >= d)(functools.partial(block, d))
    block(0)

    coupling = jnp.zeros((rows, 1), F32)
    low = []
    for g in range(kv_heads):
        for r in range(group):
            h = g * group + r
            part = (dq[g, r * rows : (r + 1) * rows, :] * scale).astype(BF)
            low.append(part)
            coupling = coupling + jnp.sum(
                part.astype(F32) * q[:, h * HEAD_SIZE : (h + 1) * HEAD_SIZE].astype(F32),
                axis=1,
                keepdims=True,
            )
    dq_low = jnp.concatenate(low, axis=1)
    owners = (diag, cross, partner, t)

    def piece_rows(n):
        return pl.ds(pl.multiple_of(owners[n] * width, 32), width)

    def query_piece(n):
        pacc[n] = dot(dq_low, wq[piece_rows(n), :], NT)

    c_wq.wait()
    done = 0
    for d in range(reach - 1, 0, -1):

        @pl.when(has_up & (i >= d))
        def _():
            dv_copy(d + 1).wait_recv()
            snd_v[d] = (part_v[d] + rcv_v[d].astype(F32)).astype(BF)
            dv_copy(d).start()
            dk_copy(d + 1).wait_recv()
            snd_k[d] = (part_k[d] + rcv_k[d].astype(F32)).astype(BF)
            dk_copy(d).start()

        if done < 4:
            query_piece(done)
            done += 1
    while done < 4:
        query_piece(done)
        done += 1
    c_wk.wait()
    c_wv.wait()
    if reach >= 1:

        @pl.when(has_up)
        def _():
            dv_copy(1).wait_recv()
            part_v[0] += rcv_v[0].astype(F32)
            dk_copy(1).wait_recv()
            part_k[0] += rcv_k[0].astype(F32)

    dk_low = (part_k[0] * scale).astype(BF)
    dv_low = part_v[0].astype(BF)
    coupling = coupling + jnp.sum(
        dk_low.astype(F32) * kb[0].astype(F32) + dv_low.astype(F32) * vb[0].astype(F32),
        axis=1,
        keepdims=True,
    )

    def piece(n):
        sl = piece_rows(n)
        return pacc[n] + dot(dk_low, wk[sl, :], NT) + dot(dv_low, wv[sl, :], NT)

    tail = rs_a.shape[1] - width
    wide = jnp.broadcast_to(coupling, (rows, tail))
    chunk = rows // ROW_CHUNKS

    send_a = remote(rs_a, rs_ar, rs_s.at[0], rs_rv.at[0], {"tp": partner})
    send_c = remote(rs_c, rs_cr, rs_s.at[1], rs_rv.at[1], {"tp": partner})

    def b_copy(n):
        sl = pl.ds(n * chunk, chunk)
        return remote(
            rs_b.at[sl], rs_br.at[sl], rs_s.at[2 + n], rs_rv.at[2 + n], {"tp": cross}
        )

    def x_copy(n):
        sl = pl.ds(n * chunk, chunk)
        return remote(res.at[sl], out_h.at[sl], x_s.at[n], x_r.at[n], {"pipe": prev})

    rs_a[:, :width] = piece(0).astype(BF)
    rs_a[:, width:] = wide.astype(BF)
    send_a.start()
    pacc[1] = piece(1)
    send_a.wait_recv()
    for n in range(ROW_CHUNKS):
        sl = slice(n * chunk, (n + 1) * chunk)
        rs_b[sl, :width] = (pacc[1, sl] + rs_ar[sl, :width].astype(F32)).astype(BF)
        rs_b[sl, width:] = (wide[sl] + rs_ar[sl, width:].astype(F32)).astype(BF)
        b_copy(n).start()
    rs_c[:, :width] = piece(2).astype(BF)
    rs_c[:, width:] = wide.astype(BF)
    send_c.start()
    pacc[3] = piece(3)
    c_xin.wait()
    c_inv.wait()
    c_gain.wait()
    inv_col = jnp.broadcast_to(inv[...], (rows, rows)).T[:, :1]
    send_c.wait_recv()
    for n in range(ROW_CHUNKS):
        sl = slice(n * chunk, (n + 1) * chunk)
        b_copy(n).wait_recv()
        normed = pacc[3, sl] + rs_cr[sl, :width].astype(F32) + rs_br[sl, :width].astype(F32)
        coup = (
            coupling[sl]
            + rs_cr[sl, width : width + 1].astype(F32)
            + rs_br[sl, width : width + 1].astype(F32)
        )
        iv = inv_col[sl]
        upl = gath[t, sl, :].astype(F32)
        val = upl + iv * (
            gain[...] * normed - xin[sl, :].astype(F32) * (iv * coup / model_width)
        )
        res[sl, :] = val.astype(BF)
        if pipe_n > 1:
            x_copy(n).start()
        else:
            pltpu.make_async_copy(
                res.at[pl.ds(n * chunk, chunk)], out_h.at[pl.ds(n * chunk, chunk)], x_s.at[n]
            ).start()

    ag_cross.wait_send()
    ag_part.wait_send()
    ag_fwd.wait_send()
    for d in range(reach):

        @pl.when(has_up & (i >= d))
        def _():
            k_copy(d).wait_send()
            v_copy(d).wait_send()

    for d in range(1, reach + 1):

        @pl.when(i >= d)
        def _():
            dv_copy(d).wait_send()
            dk_copy(d).wait_send()

    send_a.wait_send()
    send_c.wait_send()
    for n in range(ROW_CHUNKS):
        b_copy(n).wait_send()
    for n in range(ROW_CHUNKS):
        if pipe_n > 1:
            x_copy(n).wait()
        else:
            pltpu.make_async_copy(
                res.at[pl.ds(n * chunk, chunk)], out_h.at[pl.ds(n * chunk, chunk)], x_s.at[n]
            ).wait()


def per_device(up, xin, inv, gain, q, k, v, ao, wq, wk, wv, wo, lens):
    ctx_n = lax.axis_size("ctx")
    pipe_n = lax.axis_size("pipe")
    tp_n = lax.axis_size("tp")
    assert tp_n == 4
    up, xin, q, k, v, ao = up[0], xin[0], q[0], k[0], v[0], ao[0]
    wq, wk, wv, wo = wq[0], wk[0], wv[0], wo[0]
    rows, width = up.shape
    reach = min((WINDOW - 2 + rows) // rows, ctx_n - 1)
    kv_cols, q_cols = k.shape[1], q.shape[1]
    kv_heads = kv_cols // HEAD_SIZE
    stacked = rows * (q_cols // kv_cols)
    pad = (width + 127) // 128 * 128
    if pad == width:
        pad += 128
    vm = pltpu.VMEM
    dma = pltpu.SemaphoreType.DMA
    blocks = reach + 1
    scratch = [
        vm((tp_n, rows, width), BF),
        vm((rows, width), BF),
        vm(inv.shape, F32),
        vm(gain.shape, F32),
        vm(q.shape, BF),
        vm((blocks, rows, kv_cols), BF),
        vm((blocks, rows, kv_cols), BF),
        vm(ao.shape, BF),
        vm(wq.shape, BF),
        vm(wk.shape, BF),
        vm(wv.shape, BF),
        vm(wo.shape, BF),
        pltpu.SMEM(lens.shape, jnp.int32),
        vm(q.shape, BF),
        vm((kv_heads, stacked, HEAD_SIZE), BF),
        vm((kv_heads, stacked, HEAD_SIZE), BF),
        vm((blocks, kv_heads, rows, stacked), F32),
        vm((blocks, rows, kv_cols), F32),
        vm((blocks, rows, kv_cols), F32),
        vm((blocks, rows, kv_cols), BF),
        vm((blocks, rows, kv_cols), BF),
        vm((blocks, rows, kv_cols), BF),
        vm((blocks, rows, kv_cols), BF),
        vm((kv_heads, stacked, HEAD_SIZE), F32),
        vm((tp_n, rows, width), F32),
    ]
    scratch += [vm((rows, pad), BF)] * 6
    scratch += [vm((rows, width), BF)]
    scratch += [dma((13,))]
    scratch += [dma((blocks,))] * 4
    scratch += [dma((3,))] * 2
    scratch += [dma((blocks,))] * 4
    scratch += [dma((2 + ROW_CHUNKS,))] * 2
    scratch += [dma((ROW_CHUNKS,))] * 2
    out = pl.pallas_call(
        functools.partial(kernel, ctx_n, pipe_n, reach),
        out_shape=jax.ShapeDtypeStruct((rows, width), BF),
        in_specs=[pl.BlockSpec(memory_space=pl.ANY)] * 13,
        out_specs=pl.BlockSpec(memory_space=pl.ANY),
        scratch_shapes=scratch,
        compiler_params=pltpu.CompilerParams(collective_id=0, has_side_effects=True),
        name="layer_backward",
    )(up, xin, inv, gain, q, k, v, ao, wq, wk, wv, wo, lens)
    return out[None]


def solution(mesh):
    placed = (
        P("pipe", "ctx", "tp"),
        P("pipe", "ctx", "tp"),
        P("pipe", "ctx"),
        P("pipe", "tp"),
        P("pipe", "ctx", "tp"),
        P("pipe", "ctx", "tp"),
        P("pipe", "ctx", "tp"),
        P("pipe", "ctx", "tp"),
        P("pipe", None, "tp"),
        P("pipe", None, "tp"),
        P("pipe", None, "tp"),
        P("pipe", "tp", None),
        P("pipe"),
    )
    return jax.shard_map(
        per_device, mesh=mesh, in_specs=placed, out_specs=P("pipe", "ctx", "tp"), check_vma=False
    )
```

```python
import functools

import jax
import jax.numpy as jnp
from jax import lax
from jax.experimental import pallas as pl
from jax.experimental.pallas import tpu as pltpu
from jax.sharding import PartitionSpec as P

QUERY_HEADS = 16
KEY_VALUE_HEADS = 8
HEAD_SIZE = 128
WINDOW = 1024
QUERY_SCALAR = 168
NEG_FILL = -1e30
GATHER_PARTS = 2
COUPLING_ROWS = 16
NT = (((1,), (1,)), ((), ()))
NN = (((1,), (0,)), ((), ()))
TN = (((0,), (0,)), ((), ()))
BF = jnp.bfloat16
F32 = jnp.float32


def chunk_count(width):
    for n in (6, 4, 3, 2):
        if width % (16 * n) == 0:
            return n
    return 1


def dot(a, b, dims):
    return lax.dot_general(a, b, dims, preferred_element_type=F32)


def kernel(
    ctx_n,
    pipe_n,
    reach,
    up_h,
    xin_h,
    inv_h,
    gain_h,
    q_h,
    k_h,
    v_h,
    ao_h,
    wq_h,
    wk_h,
    wv_h,
    wo_h,
    len_h,
    out_h,
    gath,
    xin,
    inv,
    gain,
    q,
    kb,
    vb,
    ao,
    wq,
    wk,
    wv,
    wo,
    slen,
    wo_cut,
    gain_col,
    ao_t,
    q_t,
    k_t,
    do_t,
    s,
    part_k,
    part_v,
    snd_k,
    snd_v,
    rcv_k,
    rcv_v,
    dq,
    pacc,
    rs_a,
    rs_ar,
    rs_b,
    rs_br,
    rs_c,
    rs_cr,
    res,
    lsem,
    k_s,
    k_r,
    v_s,
    v_r,
    ag_s,
    ag_r,
    dk_s,
    dk_r,
    dv_s,
    dv_r,
    rs_s,
    rs_rv,
    x_s,
    x_r,
):
    i = lax.axis_index("ctx")
    p = lax.axis_index("pipe")
    t = lax.axis_index("tp")
    partner = t + 1 - 2 * (t % 2)
    cross = (t + 2) % 4
    diag = 3 - t
    rows = q.shape[0]
    width = xin.shape[0]
    kv_heads = kb.shape[2] // HEAD_SIZE
    group = q.shape[1] // kb.shape[2]
    stacked = group * rows
    scale = QUERY_SCALAR ** (-0.5)
    model_width = width * 4
    chunks = chunk_count(width)
    chunk = width // chunks

    def local(src, dst, n):
        c = pltpu.make_async_copy(src, dst, lsem.at[n])
        c.start()
        return c

    def remote(src, dst, ss, rs, dev):
        return pltpu.make_async_remote_copy(
            src_ref=src,
            dst_ref=dst,
            send_sem=ss,
            recv_sem=rs,
            device_id=dev,
            device_id_type=pl.DeviceIdType.MESH,
        )

    barrier = pltpu.get_barrier_semaphore()

    def greet(dev):
        pl.semaphore_signal(
            barrier, inc=1, device_id=dev, device_id_type=pl.DeviceIdType.MESH
        )

    has_up = i + 1 < ctx_n
    has_down = i > 0

    @pl.when(has_up)
    def _():
        greet({"ctx": i + 1})

    @pl.when(has_down)
    def _():
        greet({"ctx": i - 1})

    greet({"tp": partner})
    greet({"tp": cross})
    expect = 2
    prev = (p + pipe_n - 1) % pipe_n
    if pipe_n > 1:
        greet({"pipe": prev})
        expect += 1
    if pipe_n > 2:
        greet({"pipe": (p + 1) % pipe_n})
        expect += 1

    c_k = local(k_h, kb.at[0], 0)
    c_q = local(q_h, q, 1)
    c_len = local(len_h, slen, 2)
    c_up = local(up_h, gath.at[t], 3)
    c_wo = local(wo_h, wo, 5)
    c_ao = local(ao_h, ao, 6)
    c_gain = local(gain_h, gain, 12)
    c_v = local(v_h, vb.at[0], 4)
    c_wq = local(wq_h, wq, 7)
    c_wk = local(wk_h, wk, 8)
    c_wv = local(wv_h, wv, 9)
    c_xin = local(xin_h, xin, 10)
    c_inv = local(inv_h, inv, 11)

    pl.semaphore_wait(
        barrier, expect + jnp.where(has_up, 1, 0) + jnp.where(has_down, 1, 0)
    )

    up_dev = {"ctx": i + 1}
    down_dev = {"ctx": i - 1}

    def k_copy(d):
        src = k_h if d == 0 else kb.at[d]
        return remote(src, kb.at[d + 1], k_s.at[d], k_r.at[d + 1], up_dev)

    def v_copy(d):
        src = v_h if d == 0 else vb.at[d]
        return remote(src, vb.at[d + 1], v_s.at[d], v_r.at[d + 1], up_dev)

    half = width // GATHER_PARTS

    def ag_cross(n):
        sl = pl.ds(n * half, half)
        return remote(up_h.at[sl], gath.at[t, sl], ag_s.at[n], ag_r.at[n], {"tp": cross})

    def ag_fwd(n):
        sl = pl.ds(n * half, half)
        m = GATHER_PARTS + n
        return remote(
            gath.at[cross, sl], gath.at[cross, sl], ag_s.at[m], ag_r.at[m], {"tp": partner}
        )

    own_slot = 2 * GATHER_PARTS
    ag_part = remote(
        up_h, gath.at[t], ag_s.at[own_slot], ag_r.at[own_slot], {"tp": partner}
    )
    for n in range(GATHER_PARTS):
        ag_cross(n).start()

    @pl.when(has_up)
    def _():
        k_copy(0).start()
        v_copy(0).start()

    ag_part.start()

    c_len.wait()
    length = slen[0]
    key_i = lax.broadcasted_iota(jnp.int32, (rows, stacked), 0)
    qry_i = lax.broadcasted_iota(jnp.int32, (rows, stacked), 1) % rows
    later0 = qry_i - key_i
    pos_q = i * rows + qry_i
    live = pos_q < length

    def head_cols(h):
        return slice(h * HEAD_SIZE, (h + 1) * HEAD_SIZE)

    def flip(x):
        return x.astype(F32).T

    def scores(d):
        later = later0 + d * rows
        pos_k = pos_q - later
        ok = (later >= 0) & (later < WINDOW) & (pos_k < length) & live
        for g in range(kv_heads):
            keys = kb[d, :, head_cols(g)]
            sc = dot(keys, q_t[g], NN) * scale
            s[d, g] = jnp.where(ok, sc, NEG_FILL)
            k_t[d, g] = flip(keys).astype(BF)

    c_q.wait()
    for g in range(kv_heads):
        for r in range(group):
            q_t[g, :, r * rows : (r + 1) * rows] = flip(q[:, head_cols(g * group + r)]).astype(BF)
    c_k.wait()
    scores(0)
    c_ao.wait()
    for h in range(kv_heads * group):
        ao_t[head_cols(h), :] = flip(ao[:, head_cols(h)])
    c_wo.wait()
    for n in range(4):
        wo_cut[n] = wo[:, n * width : (n + 1) * width]
    c_gain.wait()
    gain_col[...] = jnp.broadcast_to(gain[...], (rows, width)).T

    def take_k(d):
        @pl.when(i >= d)
        def _():
            k_copy(d - 1).wait_recv()
            if d < reach:

                @pl.when(has_up)
                def _():
                    k_copy(d).start()

            scores(d)

    def pass_v(d):
        if d < reach:

            @pl.when(has_up & (i >= d))
            def _():
                v_copy(d - 1).wait_recv()
                v_copy(d).start()

    def need_v(d):
        if d < reach:

            @pl.when(i + 1 >= ctx_n)
            def _():
                v_copy(d - 1).wait_recv()

        else:
            v_copy(d - 1).wait_recv()

    c_up.wait()
    acc = dot(wo_cut[t], gath[t], NN)
    if reach >= 1:
        take_k(1)
    ag_cross(0).wait_recv()
    ag_fwd(0).start()
    if reach >= 1:
        pass_v(1)
    for n in range(1, GATHER_PARTS):
        ag_cross(n).wait_recv()
        ag_fwd(n).start()
    for d in range(2, reach + 1):
        take_k(d)
        pass_v(d)
    ag_part.wait_recv()
    acc = acc + dot(wo_cut[partner], gath[partner], NN)
    acc = acc + dot(wo_cut[cross], gath[cross], NN)

    for d in range(1, reach + 1):

        @pl.when(i < d)
        def _():
            s[d] = jnp.full(s.shape[1:], NEG_FILL, F32)

    for g in range(kv_heads):
        top = jnp.max(s[0, g], axis=0, keepdims=True)
        for d in range(1, reach + 1):
            top = jnp.maximum(top, jnp.max(s[d, g], axis=0, keepdims=True))
        total = jnp.zeros((1, stacked), F32)
        for d in range(reach + 1):
            val = s[d, g]
            e = jnp.where(val > 0.5 * NEG_FILL, jnp.exp(val - top), 0.0)
            s[d, g] = e
            total = total + jnp.sum(e, axis=0, keepdims=True)
        inv_total = 1.0 / jnp.where(live[:1], total, 1.0)
        for d in range(reach + 1):
            s[d, g] = s[d, g] * inv_total

    for n in range(GATHER_PARTS):
        ag_fwd(n).wait_recv()
    acc = acc + dot(wo_cut[diag], gath[diag], NN)
    grad = acc.astype(BF)
    deltas = []
    for g in range(kv_heads):
        sums = []
        for r in range(group):
            h = g * group + r
            part = grad[head_cols(h)]
            do_t[g, :, r * rows : (r + 1) * rows] = part
            sums.append(
                jnp.sum(part.astype(F32) * ao_t[head_cols(h), :], axis=0, keepdims=True)
            )
        deltas.append(jnp.concatenate(sums, axis=1))

    def dk_copy(d):
        return remote(snd_k.at[d], rcv_k.at[d - 1], dk_s.at[d], dk_r.at[d - 1], down_dev)

    def dv_copy(d):
        return remote(snd_v.at[d], rcv_v.at[d - 1], dv_s.at[d], dv_r.at[d - 1], down_dev)

    dq[...] = jnp.zeros_like(dq)

    def first_of_chain(d):
        return i + 1 >= ctx_n if d < reach else i >= d

    def block(d):
        for g in range(kv_heads):
            part_v[d, :, head_cols(g)] = dot(s[d, g].astype(BF), do_t[g], NT)
        if d > 0:

            @pl.when(first_of_chain(d))
            def _():
                snd_v[d] = part_v[d].astype(BF)
                dv_copy(d).start()

            need_v(d)
        for g in range(kv_heads):
            dprob = dot(vb[d, :, head_cols(g)], do_t[g], NN)
            ds = (s[d, g] * (dprob - deltas[g])).astype(BF)
            part_k[d, :, head_cols(g)] = dot(ds, q_t[g], NT)
            dq[g] += dot(k_t[d, g], ds, NN)
        if d > 0:

            @pl.when(first_of_chain(d))
            def _():
                snd_k[d] = part_k[d].astype(BF)
                dk_copy(d).start()

    for d in range(reach, 0, -1):
        pl.when(i >= d)(functools.partial(block, d))
    c_v.wait()
    block(0)

    coupling = jnp.zeros((1, rows), F32)
    low = []
    for g in range(kv_heads):
        for r in range(group):
            cols = slice(r * rows, (r + 1) * rows)
            part = (dq[g, :, cols] * scale).astype(BF)
            low.append(part)
            coupling = coupling + jnp.sum(
                part.astype(F32) * q_t[g, :, cols].astype(F32), axis=0, keepdims=True
            )
    dq_low = jnp.concatenate(low, axis=0)
    owners = (diag, cross, partner, t)

    def piece_rows(n):
        return pl.ds(pl.multiple_of(owners[n] * width, 16), width)

    def query_piece(n):
        pacc[n] = dot(wq[piece_rows(n), :], dq_low, NN)

    c_wq.wait()
    done = 0
    for d in range(reach - 1, 0, -1):

        @pl.when(has_up & (i >= d))
        def _():
            dv_copy(d + 1).wait_recv()
            snd_v[d] = (part_v[d] + rcv_v[d].astype(F32)).astype(BF)
            dv_copy(d).start()
            dk_copy(d + 1).wait_recv()
            snd_k[d] = (part_k[d] + rcv_k[d].astype(F32)).astype(BF)
            dk_copy(d).start()

        if done < 4:
            query_piece(done)
            done += 1
    while done < 4:
        query_piece(done)
        done += 1
    c_wk.wait()
    c_wv.wait()
    c_xin.wait()
    c_inv.wait()
    if reach >= 1:

        @pl.when(has_up)
        def _():
            dv_copy(1).wait_recv()
            part_v[0] += rcv_v[0].astype(F32)

    dv_low = part_v[0].astype(BF)
    for n in range(4):
        pacc[n] += dot(wv[piece_rows(n), :], dv_low, NT)
    if reach >= 1:

        @pl.when(has_up)
        def _():
            dk_copy(1).wait_recv()
            part_k[0] += rcv_k[0].astype(F32)

    dk_low = (part_k[0] * scale).astype(BF)
    both = dk_low.astype(F32) * kb[0].astype(F32) + dv_low.astype(F32) * vb[0].astype(F32)
    for g in range(kv_heads):
        coupling = coupling + jnp.sum(both[:, head_cols(g)].T, axis=0, keepdims=True)

    def piece(n):
        return pacc[n] + dot(wk[piece_rows(n), :], dk_low, NT)

    lead = COUPLING_ROWS
    wide = jnp.broadcast_to(coupling, (lead, rows))

    send_a = remote(rs_a, rs_ar, rs_s.at[0], rs_rv.at[0], {"tp": partner})
    send_c = remote(rs_c, rs_cr, rs_s.at[1], rs_rv.at[1], {"tp": partner})

    def b_copy(n):
        sl = pl.ds(0, lead + chunk) if n == 0 else pl.ds(lead + n * chunk, chunk)
        return remote(
            rs_b.at[sl], rs_br.at[sl], rs_s.at[2 + n], rs_rv.at[2 + n], {"tp": cross}
        )

    def x_copy(n):
        sl = pl.ds(n * chunk, chunk)
        if pipe_n == 1:
            return pltpu.make_async_copy(res.at[sl], out_h.at[sl], x_s.at[n])
        return remote(res.at[sl], out_h.at[sl], x_s.at[n], x_r.at[n], {"pipe": prev})

    rs_a[lead:, :] = piece(0).astype(BF)
    rs_a[:lead, :] = wide.astype(BF)
    send_a.start()
    pacc[1] = piece(1)
    send_a.wait_recv()
    rs_b[:lead, :] = (wide + rs_ar[:lead, :].astype(F32)).astype(BF)
    for n in range(chunks):
        sl = slice(n * chunk, (n + 1) * chunk)
        sh = slice(lead + n * chunk, lead + (n + 1) * chunk)
        rs_b[sh, :] = (pacc[1, sl] + rs_ar[sh, :].astype(F32)).astype(BF)
        b_copy(n).start()
    rs_c[lead:, :] = piece(2).astype(BF)
    rs_c[:lead, :] = wide.astype(BF)
    send_c.start()
    pacc[3] = piece(3)
    iv = inv[...]
    send_c.wait_recv()
    for n in range(chunks):
        sl = slice(n * chunk, (n + 1) * chunk)
        sh = slice(lead + n * chunk, lead + (n + 1) * chunk)
        b_copy(n).wait_recv()
        if n == 0:
            coup = (
                coupling + rs_cr[:lead, :].astype(F32)[:1] + rs_br[:lead, :].astype(F32)[:1]
            )
            drag = iv * coup / model_width
        normed = pacc[3, sl] + rs_cr[sh, :].astype(F32) + rs_br[sh, :].astype(F32)
        val = gath[t, sl, :].astype(F32) + iv * (
            gain_col[sl, :] * normed - xin[sl, :].astype(F32) * drag
        )
        res[sl, :] = val.astype(BF)
        x_copy(n).start()

    for n in range(GATHER_PARTS):
        ag_cross(n).wait_send()
        ag_fwd(n).wait_send()
    ag_part.wait_send()
    for d in range(reach):

        @pl.when(has_up & (i >= d))
        def _():
            k_copy(d).wait_send()
            v_copy(d).wait_send()

    for d in range(1, reach + 1):

        @pl.when(i >= d)
        def _():
            dv_copy(d).wait_send()
            dk_copy(d).wait_send()

    send_a.wait_send()
    send_c.wait_send()
    for n in range(chunks):
        b_copy(n).wait_send()
    for n in range(chunks):
        x_copy(n).wait()


def per_device(up, xin, inv, gain, q, k, v, ao, wq, wk, wv, wo, lens):
    ctx_n = lax.axis_size("ctx")
    pipe_n = lax.axis_size("pipe")
    tp_n = lax.axis_size("tp")
    assert tp_n == 4
    up, xin, q, k, v, ao = up[0].T, xin[0].T, q[0], k[0], v[0], ao[0]
    wq, wk, wv, wo = wq[0], wk[0], wv[0], wo[0]
    width, rows = up.shape
    reach = min((WINDOW - 2 + rows) // rows, ctx_n - 1)
    kv_cols, q_cols = k.shape[1], q.shape[1]
    kv_heads = kv_cols // HEAD_SIZE
    stacked = rows * (q_cols // kv_cols)
    chunks = chunk_count(width)
    vm = pltpu.VMEM
    dma = pltpu.SemaphoreType.DMA
    blocks = reach + 1
    scratch = [
        vm((tp_n, width, rows), BF),
        vm((width, rows), BF),
        vm(inv.shape, F32),
        vm(gain.shape, F32),
        vm(q.shape, BF),
        vm((blocks, rows, kv_cols), BF),
        vm((blocks, rows, kv_cols), BF),
        vm(ao.shape, BF),
        vm(wq.shape, BF),
        vm(wk.shape, BF),
        vm(wv.shape, BF),
        vm(wo.shape, BF),
        pltpu.SMEM(lens.shape, jnp.int32),
        vm((tp_n, wo.shape[0], width), BF),
        vm((width, rows), F32),
        vm((q_cols, rows), F32),
        vm((kv_heads, HEAD_SIZE, stacked), BF),
        vm((blocks, kv_heads, HEAD_SIZE, rows), BF),
        vm((kv_heads, HEAD_SIZE, stacked), BF),
        vm((blocks, kv_heads, rows, stacked), F32),
        vm((blocks, rows, kv_cols), F32),
        vm((blocks, rows, kv_cols), F32),
        vm((blocks, rows, kv_cols), BF),
        vm((blocks, rows, kv_cols), BF),
        vm((blocks, rows, kv_cols), BF),
        vm((blocks, rows, kv_cols), BF),
        vm((kv_heads, HEAD_SIZE, stacked), F32),
        vm((tp_n, width, rows), F32),
    ]
    scratch += [vm((COUPLING_ROWS + width, rows), BF)] * 6
    scratch += [vm((width, rows), BF)]
    scratch += [dma((13,))]
    scratch += [dma((blocks,))] * 4
    scratch += [dma((2 * GATHER_PARTS + 1,))] * 2
    scratch += [dma((blocks,))] * 4
    scratch += [dma((2 + chunks,))] * 2
    scratch += [dma((chunks,))] * 2
    out = pl.pallas_call(
        functools.partial(kernel, ctx_n, pipe_n, reach),
        out_shape=jax.ShapeDtypeStruct((width, rows), BF),
        in_specs=[pl.BlockSpec(memory_space=pl.ANY)] * 13,
        out_specs=pl.BlockSpec(memory_space=pl.ANY),
        scratch_shapes=scratch,
        compiler_params=pltpu.CompilerParams(collective_id=0, has_side_effects=True),
        name="layer_backward",
    )(up, xin, inv, gain, q, k, v, ao, wq, wk, wv, wo, lens)
    return out.T[None]


def solution(mesh):
    placed = (
        P("pipe", "ctx", "tp"),
        P("pipe", "ctx", "tp"),
        P("pipe", "ctx"),
        P("pipe", "tp"),
        P("pipe", "ctx", "tp"),
        P("pipe", "ctx", "tp"),
        P("pipe", "ctx", "tp"),
        P("pipe", "ctx", "tp"),
        P("pipe", None, "tp"),
        P("pipe", None, "tp"),
        P("pipe", None, "tp"),
        P("pipe", "tp", None),
        P("pipe"),
    )
    return jax.shard_map(
        per_device, mesh=mesh, in_specs=placed, out_specs=P("pipe", "ctx", "tp"), check_vma=False
    )
```

```python
import functools

import jax
import jax.numpy as jnp
from jax import lax
from jax.experimental import pallas as pl
from jax.experimental.pallas import tpu as pltpu
from jax.sharding import PartitionSpec as P

QUERY_HEADS = 16
KEY_VALUE_HEADS = 8
HEAD_SIZE = 128
WINDOW = 1024
QUERY_SCALAR = 168
NEG_FILL = -1e30
GATHER_PARTS = 2
COUPLING_ROWS = 16
NT = (((1,), (1,)), ((), ()))
NN = (((1,), (0,)), ((), ()))
TN = (((0,), (0,)), ((), ()))
BF = jnp.bfloat16
F32 = jnp.float32


def chunk_count(width):
    for n in (6, 4, 3, 2):
        if width % (16 * n) == 0:
            return n
    return 1


def dot(a, b, dims):
    return lax.dot_general(a, b, dims, preferred_element_type=F32)


def kernel(
    ctx_n,
    pipe_n,
    reach,
    up_h,
    xin_h,
    inv_h,
    gain_h,
    q_h,
    k_h,
    v_h,
    ao_h,
    wq_h,
    wk_h,
    wv_h,
    wo_h,
    len_h,
    out_h,
    gath,
    xin,
    inv,
    gain,
    q,
    kb,
    vb,
    ao,
    wq,
    wk,
    wv,
    wo,
    slen,
    wo_cut,
    gain_col,
    ao_t,
    q_t,
    k_t,
    do_t,
    s,
    part_k,
    part_v,
    snd_k,
    snd_v,
    rcv_k,
    rcv_v,
    dq,
    pacc,
    rs_a,
    rs_ar,
    rs_b,
    rs_br,
    rs_c,
    rs_cr,
    res,
    lsem,
    k_s,
    k_r,
    v_s,
    v_r,
    ag_s,
    ag_r,
    dk_s,
    dk_r,
    dv_s,
    dv_r,
    rs_s,
    rs_rv,
    x_s,
    x_r,
):
    i = lax.axis_index("ctx")
    p = lax.axis_index("pipe")
    t = lax.axis_index("tp")
    partner = t + 1 - 2 * (t % 2)
    cross = (t + 2) % 4
    diag = 3 - t
    rows = q.shape[0]
    width = xin.shape[0]
    kv_heads = kb.shape[2] // HEAD_SIZE
    group = q.shape[1] // kb.shape[2]
    stacked = group * rows
    scale = QUERY_SCALAR ** (-0.5)
    model_width = width * 4
    chunks = chunk_count(width)
    chunk = width // chunks

    def local(src, dst, n):
        c = pltpu.make_async_copy(src, dst, lsem.at[n])
        c.start()
        return c

    def remote(src, dst, ss, rs, dev):
        return pltpu.make_async_remote_copy(
            src_ref=src,
            dst_ref=dst,
            send_sem=ss,
            recv_sem=rs,
            device_id=dev,
            device_id_type=pl.DeviceIdType.MESH,
        )

    barrier = pltpu.get_barrier_semaphore()

    def greet(dev):
        pl.semaphore_signal(
            barrier, inc=1, device_id=dev, device_id_type=pl.DeviceIdType.MESH
        )

    has_up = i + 1 < ctx_n
    has_down = i > 0

    @pl.when(has_up)
    def _():
        greet({"ctx": i + 1})

    @pl.when(has_down)
    def _():
        greet({"ctx": i - 1})

    greet({"tp": partner})
    greet({"tp": cross})
    expect = 2
    prev = (p + pipe_n - 1) % pipe_n
    if pipe_n > 1:
        greet({"pipe": prev})
        expect += 1
    if pipe_n > 2:
        greet({"pipe": (p + 1) % pipe_n})
        expect += 1

    c_k = local(k_h, kb.at[0], 0)
    c_q = local(q_h, q, 1)
    c_len = local(len_h, slen, 2)
    c_up = local(up_h, gath.at[t], 3)
    c_wo = local(wo_h, wo, 5)
    c_ao = local(ao_h, ao, 6)
    c_gain = local(gain_h, gain, 12)
    c_v = local(v_h, vb.at[0], 4)
    c_wq = local(wq_h, wq, 7)
    c_wk = local(wk_h, wk, 8)
    c_wv = local(wv_h, wv, 9)
    c_xin = local(xin_h, xin, 10)
    c_inv = local(inv_h, inv, 11)

    pl.semaphore_wait(
        barrier, expect + jnp.where(has_up, 1, 0) + jnp.where(has_down, 1, 0)
    )

    up_dev = {"ctx": i + 1}
    down_dev = {"ctx": i - 1}

    def k_copy(d):
        src = k_h if d == 0 else kb.at[d]
        return remote(src, kb.at[d + 1], k_s.at[d], k_r.at[d + 1], up_dev)

    def v_copy(d):
        src = v_h if d == 0 else vb.at[d]
        return remote(src, vb.at[d + 1], v_s.at[d], v_r.at[d + 1], up_dev)

    half = width // GATHER_PARTS

    def ag_cross(n):
        sl = pl.ds(n * half, half)
        return remote(up_h.at[sl], gath.at[t, sl], ag_s.at[n], ag_r.at[n], {"tp": cross})

    def ag_fwd(n):
        sl = pl.ds(n * half, half)
        m = GATHER_PARTS + n
        return remote(
            gath.at[cross, sl], gath.at[cross, sl], ag_s.at[m], ag_r.at[m], {"tp": partner}
        )

    own_slot = 2 * GATHER_PARTS
    ag_part = remote(
        up_h, gath.at[t], ag_s.at[own_slot], ag_r.at[own_slot], {"tp": partner}
    )
    for n in range(GATHER_PARTS):
        ag_cross(n).start()

    @pl.when(has_up)
    def _():
        k_copy(0).start()
        v_copy(0).start()

    ag_part.start()

    c_len.wait()
    length = slen[0]
    key_i = lax.broadcasted_iota(jnp.int32, (rows, stacked), 0)
    qry_i = lax.broadcasted_iota(jnp.int32, (rows, stacked), 1) % rows
    later0 = qry_i - key_i
    pos_q = i * rows + qry_i
    live = pos_q < length

    def head_cols(h):
        return slice(h * HEAD_SIZE, (h + 1) * HEAD_SIZE)

    def flip(x):
        return x.astype(F32).T

    def scores(d):
        later = later0 + d * rows
        pos_k = pos_q - later
        ok = (later >= 0) & (later < WINDOW) & (pos_k < length) & live
        for g in range(kv_heads):
            keys = kb[d, :, head_cols(g)]
            sc = dot(keys, q_t[g], NN) * scale
            s[d, g] = jnp.where(ok, sc, NEG_FILL)
            k_t[d, g] = flip(keys).astype(BF)

    c_q.wait()
    for g in range(kv_heads):
        for r in range(group):
            q_t[g, :, r * rows : (r + 1) * rows] = flip(q[:, head_cols(g * group + r)]).astype(BF)
    c_k.wait()
    scores(0)
    c_ao.wait()
    for h in range(kv_heads * group):
        ao_t[head_cols(h), :] = flip(ao[:, head_cols(h)])
    c_wo.wait()
    for n in range(4):
        wo_cut[n] = wo[:, n * width : (n + 1) * width]
    c_gain.wait()
    gain_col[...] = jnp.broadcast_to(gain[...], (rows, width)).T

    def take_k(d):
        @pl.when(i >= d)
        def _():
            k_copy(d - 1).wait_recv()
            if d < reach:

                @pl.when(has_up)
                def _():
                    k_copy(d).start()

            scores(d)

    def pass_v(d):
        if d < reach:

            @pl.when(has_up & (i >= d))
            def _():
                v_copy(d - 1).wait_recv()
                v_copy(d).start()

    def need_v(d):
        if d < reach:

            @pl.when(i + 1 >= ctx_n)
            def _():
                v_copy(d - 1).wait_recv()

        else:
            v_copy(d - 1).wait_recv()

    c_up.wait()
    acc = dot(wo_cut[t], gath[t], NN)
    if reach >= 1:
        take_k(1)
    ag_cross(0).wait_recv()
    ag_fwd(0).start()
    if reach >= 1:
        pass_v(1)
    for n in range(1, GATHER_PARTS):
        ag_cross(n).wait_recv()
        ag_fwd(n).start()
    for d in range(2, reach + 1):
        take_k(d)
        pass_v(d)
    ag_part.wait_recv()
    acc = acc + dot(wo_cut[partner], gath[partner], NN)
    acc = acc + dot(wo_cut[cross], gath[cross], NN)

    for d in range(1, reach + 1):

        @pl.when(i < d)
        def _():
            s[d] = jnp.full(s.shape[1:], NEG_FILL, F32)

    for g in range(kv_heads):
        top = jnp.max(s[0, g], axis=0, keepdims=True)
        for d in range(1, reach + 1):
            top = jnp.maximum(top, jnp.max(s[d, g], axis=0, keepdims=True))
        total = jnp.zeros((1, stacked), F32)
        for d in range(reach + 1):
            val = s[d, g]
            e = jnp.where(val > 0.5 * NEG_FILL, jnp.exp(val - top), 0.0)
            s[d, g] = e
            total = total + jnp.sum(e, axis=0, keepdims=True)
        inv_total = 1.0 / jnp.where(live[:1], total, 1.0)
        for d in range(reach + 1):
            s[d, g] = s[d, g] * inv_total

    for n in range(GATHER_PARTS):
        ag_fwd(n).wait_recv()
    acc = acc + dot(wo_cut[diag], gath[diag], NN)
    grad = acc.astype(BF)
    deltas = []
    for g in range(kv_heads):
        sums = []
        for r in range(group):
            h = g * group + r
            part = grad[head_cols(h)]
            do_t[g, :, r * rows : (r + 1) * rows] = part
            sums.append(
                jnp.sum(part.astype(F32) * ao_t[head_cols(h), :], axis=0, keepdims=True)
            )
        deltas.append(jnp.concatenate(sums, axis=1))

    def dk_copy(d, g):
        return remote(
            snd_k.at[d, g], rcv_k.at[d - 1, g], dk_s.at[d, g], dk_r.at[d - 1, g], down_dev
        )

    def dv_copy(d, g):
        return remote(
            snd_v.at[d, g], rcv_v.at[d - 1, g], dv_s.at[d, g], dv_r.at[d - 1, g], down_dev
        )

    dq[...] = jnp.zeros_like(dq)

    def first_of_chain(d):
        return i + 1 >= ctx_n if d < reach else i >= d

    def block(d):
        for g in range(kv_heads):
            part_v[d, g] = dot(s[d, g].astype(BF), do_t[g], NT)
            if d > 0:

                @pl.when(first_of_chain(d))
                def _():
                    snd_v[d, g] = part_v[d, g].astype(BF)
                    dv_copy(d, g).start()

        if d > 0:
            need_v(d)
        for g in range(kv_heads):
            dprob = dot(vb[d, :, head_cols(g)], do_t[g], NN)
            ds = (s[d, g] * (dprob - deltas[g])).astype(BF)
            part_k[d, g] = dot(ds, q_t[g], NT)
            if d > 0:

                @pl.when(first_of_chain(d))
                def _():
                    snd_k[d, g] = part_k[d, g].astype(BF)
                    dk_copy(d, g).start()

            dq[g] += dot(k_t[d, g], ds, NN)

    for d in range(reach, 0, -1):
        pl.when(i >= d)(functools.partial(block, d))
    c_v.wait()
    block(0)

    coupling = jnp.zeros((1, rows), F32)
    low = []
    for g in range(kv_heads):
        for r in range(group):
            cols = slice(r * rows, (r + 1) * rows)
            part = (dq[g, :, cols] * scale).astype(BF)
            low.append(part)
            coupling = coupling + jnp.sum(
                part.astype(F32) * q_t[g, :, cols].astype(F32), axis=0, keepdims=True
            )
    dq_low = jnp.concatenate(low, axis=0)
    owners = (diag, cross, partner, t)

    def piece_rows(n):
        return pl.ds(pl.multiple_of(owners[n] * width, 16), width)

    def query_piece(n):
        pacc[n] = dot(wq[piece_rows(n), :], dq_low, NN)

    c_wq.wait()
    done = 0
    for d in range(reach - 1, 0, -1):

        @pl.when(has_up & (i >= d))
        def _():
            for g in range(kv_heads):
                dv_copy(d + 1, g).wait_recv()
                snd_v[d, g] = (part_v[d, g] + rcv_v[d, g].astype(F32)).astype(BF)
                dv_copy(d, g).start()
            for g in range(kv_heads):
                dk_copy(d + 1, g).wait_recv()
                snd_k[d, g] = (part_k[d, g] + rcv_k[d, g].astype(F32)).astype(BF)
                dk_copy(d, g).start()

        if done < 4:
            query_piece(done)
            done += 1
    while done < 4:
        query_piece(done)
        done += 1
    c_wk.wait()
    c_wv.wait()
    c_xin.wait()
    c_inv.wait()
    if reach >= 1:

        @pl.when(has_up)
        def _():
            for g in range(kv_heads):
                dv_copy(1, g).wait_recv()
                part_v[0, g] += rcv_v[0, g].astype(F32)

    dv_low = jnp.concatenate([part_v[0, g].astype(BF) for g in range(kv_heads)], axis=1)
    for n in range(4):
        pacc[n] += dot(wv[piece_rows(n), :], dv_low, NT)
    if reach >= 1:

        @pl.when(has_up)
        def _():
            for g in range(kv_heads):
                dk_copy(1, g).wait_recv()
                part_k[0, g] += rcv_k[0, g].astype(F32)

    dk_low = jnp.concatenate(
        [(part_k[0, g] * scale).astype(BF) for g in range(kv_heads)], axis=1
    )
    both = dk_low.astype(F32) * kb[0].astype(F32) + dv_low.astype(F32) * vb[0].astype(F32)
    for g in range(kv_heads):
        coupling = coupling + jnp.sum(both[:, head_cols(g)].T, axis=0, keepdims=True)

    def piece(n):
        return pacc[n] + dot(wk[piece_rows(n), :], dk_low, NT)

    lead = COUPLING_ROWS
    wide = jnp.broadcast_to(coupling, (lead, rows))

    send_a = remote(rs_a, rs_ar, rs_s.at[0], rs_rv.at[0], {"tp": partner})
    send_c = remote(rs_c, rs_cr, rs_s.at[1], rs_rv.at[1], {"tp": partner})

    def b_copy(n):
        sl = pl.ds(0, lead + chunk) if n == 0 else pl.ds(lead + n * chunk, chunk)
        return remote(
            rs_b.at[sl], rs_br.at[sl], rs_s.at[2 + n], rs_rv.at[2 + n], {"tp": cross}
        )

    def x_copy(n):
        sl = pl.ds(n * chunk, chunk)
        if pipe_n == 1:
            return pltpu.make_async_copy(res.at[sl], out_h.at[sl], x_s.at[n])
        return remote(res.at[sl], out_h.at[sl], x_s.at[n], x_r.at[n], {"pipe": prev})

    rs_a[lead:, :] = piece(0).astype(BF)
    rs_a[:lead, :] = wide.astype(BF)
    send_a.start()
    pacc[1] = piece(1)
    send_a.wait_recv()
    rs_b[:lead, :] = (wide + rs_ar[:lead, :].astype(F32)).astype(BF)
    for n in range(chunks):
        sl = slice(n * chunk, (n + 1) * chunk)
        sh = slice(lead + n * chunk, lead + (n + 1) * chunk)
        rs_b[sh, :] = (pacc[1, sl] + rs_ar[sh, :].astype(F32)).astype(BF)
        b_copy(n).start()
    rs_c[lead:, :] = piece(2).astype(BF)
    rs_c[:lead, :] = wide.astype(BF)
    send_c.start()
    pacc[3] = piece(3)
    iv = inv[...]
    send_c.wait_recv()
    for n in range(chunks):
        sl = slice(n * chunk, (n + 1) * chunk)
        sh = slice(lead + n * chunk, lead + (n + 1) * chunk)
        b_copy(n).wait_recv()
        if n == 0:
            coup = (
                coupling + rs_cr[:lead, :].astype(F32)[:1] + rs_br[:lead, :].astype(F32)[:1]
            )
            drag = iv * coup / model_width
        normed = pacc[3, sl] + rs_cr[sh, :].astype(F32) + rs_br[sh, :].astype(F32)
        val = gath[t, sl, :].astype(F32) + iv * (
            gain_col[sl, :] * normed - xin[sl, :].astype(F32) * drag
        )
        res[sl, :] = val.astype(BF)
        x_copy(n).start()

    for n in range(GATHER_PARTS):
        ag_cross(n).wait_send()
        ag_fwd(n).wait_send()
    ag_part.wait_send()
    for d in range(reach):

        @pl.when(has_up & (i >= d))
        def _():
            k_copy(d).wait_send()
            v_copy(d).wait_send()

    for d in range(1, reach + 1):

        @pl.when(i >= d)
        def _():
            for g in range(kv_heads):
                dv_copy(d, g).wait_send()
                dk_copy(d, g).wait_send()

    send_a.wait_send()
    send_c.wait_send()
    for n in range(chunks):
        b_copy(n).wait_send()
    for n in range(chunks):
        x_copy(n).wait()


def per_device(up, xin, inv, gain, q, k, v, ao, wq, wk, wv, wo, lens):
    ctx_n = lax.axis_size("ctx")
    pipe_n = lax.axis_size("pipe")
    tp_n = lax.axis_size("tp")
    assert tp_n == 4
    up, xin, q, k, v, ao = up[0].T, xin[0].T, q[0], k[0], v[0], ao[0]
    wq, wk, wv, wo = wq[0], wk[0], wv[0], wo[0]
    width, rows = up.shape
    reach = min((WINDOW - 2 + rows) // rows, ctx_n - 1)
    kv_cols, q_cols = k.shape[1], q.shape[1]
    kv_heads = kv_cols // HEAD_SIZE
    stacked = rows * (q_cols // kv_cols)
    chunks = chunk_count(width)
    vm = pltpu.VMEM
    dma = pltpu.SemaphoreType.DMA
    blocks = reach + 1
    scratch = [
        vm((tp_n, width, rows), BF),
        vm((width, rows), BF),
        vm(inv.shape, F32),
        vm(gain.shape, F32),
        vm(q.shape, BF),
        vm((blocks, rows, kv_cols), BF),
        vm((blocks, rows, kv_cols), BF),
        vm(ao.shape, BF),
        vm(wq.shape, BF),
        vm(wk.shape, BF),
        vm(wv.shape, BF),
        vm(wo.shape, BF),
        pltpu.SMEM(lens.shape, jnp.int32),
        vm((tp_n, wo.shape[0], width), BF),
        vm((width, rows), F32),
        vm((q_cols, rows), F32),
        vm((kv_heads, HEAD_SIZE, stacked), BF),
        vm((blocks, kv_heads, HEAD_SIZE, rows), BF),
        vm((kv_heads, HEAD_SIZE, stacked), BF),
        vm((blocks, kv_heads, rows, stacked), F32),
        vm((blocks, kv_heads, rows, HEAD_SIZE), F32),
        vm((blocks, kv_heads, rows, HEAD_SIZE), F32),
        vm((blocks, kv_heads, rows, HEAD_SIZE), BF),
        vm((blocks, kv_heads, rows, HEAD_SIZE), BF),
        vm((blocks, kv_heads, rows, HEAD_SIZE), BF),
        vm((blocks, kv_heads, rows, HEAD_SIZE), BF),
        vm((kv_heads, HEAD_SIZE, stacked), F32),
        vm((tp_n, width, rows), F32),
    ]
    scratch += [vm((COUPLING_ROWS + width, rows), BF)] * 6
    scratch += [vm((width, rows), BF)]
    scratch += [dma((13,))]
    scratch += [dma((blocks,))] * 4
    scratch += [dma((2 * GATHER_PARTS + 1,))] * 2
    scratch += [dma((blocks, kv_heads))] * 4
    scratch += [dma((2 + chunks,))] * 2
    scratch += [dma((chunks,))] * 2
    out = pl.pallas_call(
        functools.partial(kernel, ctx_n, pipe_n, reach),
        out_shape=jax.ShapeDtypeStruct((width, rows), BF),
        in_specs=[pl.BlockSpec(memory_space=pl.ANY)] * 13,
        out_specs=pl.BlockSpec(memory_space=pl.ANY),
        scratch_shapes=scratch,
        compiler_params=pltpu.CompilerParams(collective_id=0, has_side_effects=True),
        name="layer_backward",
    )(up, xin, inv, gain, q, k, v, ao, wq, wk, wv, wo, lens)
    return out.T[None]


def solution(mesh):
    placed = (
        P("pipe", "ctx", "tp"),
        P("pipe", "ctx", "tp"),
        P("pipe", "ctx"),
        P("pipe", "tp"),
        P("pipe", "ctx", "tp"),
        P("pipe", "ctx", "tp"),
        P("pipe", "ctx", "tp"),
        P("pipe", "ctx", "tp"),
        P("pipe", None, "tp"),
        P("pipe", None, "tp"),
        P("pipe", None, "tp"),
        P("pipe", "tp", None),
        P("pipe"),
    )
    return jax.shard_map(
        per_device, mesh=mesh, in_specs=placed, out_specs=P("pipe", "ctx", "tp"), check_vma=False
    )
```

```python
import functools

import jax
import jax.numpy as jnp
from jax import lax
from jax.experimental import pallas as pl
from jax.experimental.pallas import tpu as pltpu
from jax.sharding import PartitionSpec as P

QUERY_HEADS = 16
KEY_VALUE_HEADS = 8
HEAD_SIZE = 128
WINDOW = 1024
QUERY_SCALAR = 168
NEG_FILL = -1e30
GATHER_PARTS = 2
COUPLING_ROWS = 16
NT = (((1,), (1,)), ((), ()))
NN = (((1,), (0,)), ((), ()))
TN = (((0,), (0,)), ((), ()))
BF = jnp.bfloat16
F32 = jnp.float32


def chunk_count(width):
    for n in (6, 4, 3, 2):
        if width % (16 * n) == 0:
            return n
    return 1


def dot(a, b, dims):
    return lax.dot_general(a, b, dims, preferred_element_type=F32)


def kernel(
    ctx_n,
    pipe_n,
    reach,
    up_h,
    xin_h,
    inv_h,
    gain_h,
    q_h,
    k_h,
    v_h,
    ao_h,
    wq_h,
    wk_h,
    wv_h,
    wo_h,
    len_h,
    out_h,
    gath,
    xin,
    inv,
    gain,
    q,
    kb,
    vb,
    ao,
    wq,
    wk,
    wv,
    wo,
    slen,
    wo_cut,
    gain_col,
    ao_t,
    q_t,
    k_t,
    do_t,
    s,
    part_k,
    part_v,
    snd_k,
    snd_v,
    rcv_k,
    rcv_v,
    dq,
    pacc,
    rs_a,
    rs_ar,
    rs_b,
    rs_br,
    rs_c,
    rs_cr,
    res,
    lsem,
    k_s,
    k_r,
    v_s,
    v_r,
    ag_s,
    ag_r,
    dk_s,
    dk_r,
    dv_s,
    dv_r,
    rs_s,
    rs_rv,
    x_s,
    x_r,
):
    i = lax.axis_index("ctx")
    p = lax.axis_index("pipe")
    t = lax.axis_index("tp")
    partner = t + 1 - 2 * (t % 2)
    cross = (t + 2) % 4
    diag = 3 - t
    rows = q.shape[0]
    width = xin.shape[0]
    kv_heads = kb.shape[2] // HEAD_SIZE
    group = q.shape[1] // kb.shape[2]
    stacked = group * rows
    scale = QUERY_SCALAR ** (-0.5)
    model_width = width * 4
    chunks = chunk_count(width)
    chunk = width // chunks

    def local(src, dst, n):
        c = pltpu.make_async_copy(src, dst, lsem.at[n])
        c.start()
        return c

    def remote(src, dst, ss, rs, dev):
        return pltpu.make_async_remote_copy(
            src_ref=src,
            dst_ref=dst,
            send_sem=ss,
            recv_sem=rs,
            device_id=dev,
            device_id_type=pl.DeviceIdType.MESH,
        )

    barrier = pltpu.get_barrier_semaphore()

    def greet(dev):
        pl.semaphore_signal(
            barrier, inc=1, device_id=dev, device_id_type=pl.DeviceIdType.MESH
        )

    has_up = i + 1 < ctx_n
    has_down = i > 0

    @pl.when(has_up)
    def _():
        greet({"ctx": i + 1})

    @pl.when(has_down)
    def _():
        greet({"ctx": i - 1})

    greet({"tp": partner})
    greet({"tp": cross})
    expect = 2
    prev = (p + pipe_n - 1) % pipe_n
    if pipe_n > 1:
        greet({"pipe": prev})
        expect += 1
    if pipe_n > 2:
        greet({"pipe": (p + 1) % pipe_n})
        expect += 1

    c_k = local(k_h, kb.at[0], 0)
    c_q = local(q_h, q, 1)
    c_len = local(len_h, slen, 2)
    c_up = local(up_h, gath.at[t], 3)
    c_wo = local(wo_h, wo, 5)
    c_ao = local(ao_h, ao, 6)
    c_gain = local(gain_h, gain, 12)
    c_v = local(v_h, vb.at[0], 4)
    c_wq = local(wq_h, wq, 7)
    c_wk = local(wk_h, wk, 8)
    c_wv = local(wv_h, wv, 9)
    c_xin = local(xin_h, xin, 10)
    c_inv = local(inv_h, inv, 11)

    pl.semaphore_wait(
        barrier, expect + jnp.where(has_up, 1, 0) + jnp.where(has_down, 1, 0)
    )

    up_dev = {"ctx": i + 1}
    down_dev = {"ctx": i - 1}

    def k_copy(d):
        src = k_h if d == 0 else kb.at[d]
        return remote(src, kb.at[d + 1], k_s.at[d], k_r.at[d + 1], up_dev)

    def v_copy(d):
        src = v_h if d == 0 else vb.at[d]
        return remote(src, vb.at[d + 1], v_s.at[d], v_r.at[d + 1], up_dev)

    half = width // GATHER_PARTS

    def ag_cross(n):
        sl = pl.ds(n * half, half)
        return remote(up_h.at[sl], gath.at[t, sl], ag_s.at[n], ag_r.at[n], {"tp": cross})

    def ag_fwd(n):
        sl = pl.ds(n * half, half)
        m = GATHER_PARTS + n
        return remote(
            gath.at[cross, sl], gath.at[cross, sl], ag_s.at[m], ag_r.at[m], {"tp": partner}
        )

    own_slot = 2 * GATHER_PARTS
    ag_part = remote(
        up_h, gath.at[t], ag_s.at[own_slot], ag_r.at[own_slot], {"tp": partner}
    )
    for n in range(GATHER_PARTS):
        ag_cross(n).start()

    @pl.when(has_up)
    def _():
        k_copy(0).start()
        v_copy(0).start()

    ag_part.start()

    c_len.wait()
    length = slen[0]
    key_i = lax.broadcasted_iota(jnp.int32, (rows, stacked), 0)
    qry_i = lax.broadcasted_iota(jnp.int32, (rows, stacked), 1) % rows
    later0 = qry_i - key_i
    pos_q = i * rows + qry_i
    live = pos_q < length

    def head_cols(h):
        return slice(h * HEAD_SIZE, (h + 1) * HEAD_SIZE)

    def flip(x):
        return x.astype(F32).T

    def scores(d):
        later = later0 + d * rows
        pos_k = pos_q - later
        ok = (later >= 0) & (later < WINDOW) & (pos_k < length) & live
        for g in range(kv_heads):
            keys = kb[d, :, head_cols(g)]
            sc = dot(keys, q_t[g], NN) * scale
            s[d, g] = jnp.where(ok, sc, NEG_FILL)
            k_t[d, g] = flip(keys).astype(BF)

    c_q.wait()
    for g in range(kv_heads):
        for r in range(group):
            q_t[g, :, r * rows : (r + 1) * rows] = flip(q[:, head_cols(g * group + r)]).astype(BF)
    c_k.wait()
    scores(0)
    c_ao.wait()
    for h in range(kv_heads * group):
        ao_t[head_cols(h), :] = flip(ao[:, head_cols(h)])
    c_wo.wait()
    for n in range(4):
        wo_cut[n] = wo[:, n * width : (n + 1) * width]
    c_gain.wait()
    gain_col[...] = jnp.broadcast_to(gain[...], (rows, width)).T

    def take_k(d):
        @pl.when(i >= d)
        def _():
            k_copy(d - 1).wait_recv()
            if d < reach:

                @pl.when(has_up)
                def _():
                    k_copy(d).start()

            scores(d)

    def pass_v(d):
        if d < reach:

            @pl.when(has_up & (i >= d))
            def _():
                v_copy(d - 1).wait_recv()
                v_copy(d).start()

    def need_v(d):
        if d < reach:

            @pl.when(i + 1 >= ctx_n)
            def _():
                v_copy(d - 1).wait_recv()

        else:
            v_copy(d - 1).wait_recv()

    c_up.wait()
    acc = dot(wo_cut[t], gath[t], NN)
    if reach >= 1:
        take_k(1)
    ag_cross(0).wait_recv()
    ag_fwd(0).start()
    if reach >= 1:
        pass_v(1)
    for n in range(1, GATHER_PARTS):
        ag_cross(n).wait_recv()
        ag_fwd(n).start()
    for d in range(2, reach + 1):
        take_k(d)
        pass_v(d)
    ag_part.wait_recv()
    acc = acc + dot(wo_cut[partner], gath[partner], NN)
    acc = acc + dot(wo_cut[cross], gath[cross], NN)

    for d in range(1, reach + 1):

        @pl.when(i < d)
        def _():
            s[d] = jnp.full(s.shape[1:], NEG_FILL, F32)

    for g in range(kv_heads):
        top = jnp.max(s[0, g], axis=0, keepdims=True)
        for d in range(1, reach + 1):
            top = jnp.maximum(top, jnp.max(s[d, g], axis=0, keepdims=True))
        total = jnp.zeros((1, stacked), F32)
        for d in range(reach + 1):
            val = s[d, g]
            e = jnp.where(val > 0.5 * NEG_FILL, jnp.exp(val - top), 0.0)
            s[d, g] = e
            total = total + jnp.sum(e, axis=0, keepdims=True)
        inv_total = 1.0 / jnp.where(live[:1], total, 1.0)
        for d in range(reach + 1):
            s[d, g] = s[d, g] * inv_total

    for n in range(GATHER_PARTS):
        ag_fwd(n).wait_recv()
    acc = acc + dot(wo_cut[diag], gath[diag], NN)
    grad = acc.astype(BF)
    deltas = []
    for g in range(kv_heads):
        sums = []
        for r in range(group):
            h = g * group + r
            part = grad[head_cols(h)]
            do_t[g, :, r * rows : (r + 1) * rows] = part
            sums.append(
                jnp.sum(part.astype(F32) * ao_t[head_cols(h), :], axis=0, keepdims=True)
            )
        deltas.append(jnp.concatenate(sums, axis=1))

    def dk_copy(d, g):
        return remote(
            snd_k.at[d, g], rcv_k.at[d - 1, g], dk_s.at[d, g], dk_r.at[d - 1, g], down_dev
        )

    def dv_copy(d, g):
        return remote(
            snd_v.at[d, g], rcv_v.at[d - 1, g], dv_s.at[d, g], dv_r.at[d - 1, g], down_dev
        )

    dq[...] = jnp.zeros_like(dq)

    def first_of_chain(d):
        return i + 1 >= ctx_n if d < reach else i >= d

    def block(d):
        for g in range(kv_heads):
            part_v[d, g] = dot(s[d, g].astype(BF), do_t[g], NT)
            if d > 0:

                @pl.when(first_of_chain(d))
                def _():
                    snd_v[d, g] = part_v[d, g].astype(BF)
                    dv_copy(d, g).start()

        if d > 0:
            need_v(d)
        for g in range(kv_heads):
            dprob = dot(vb[d, :, head_cols(g)], do_t[g], NN)
            ds = (s[d, g] * (dprob - deltas[g])).astype(BF)
            part_k[d, g] = dot(ds, q_t[g], NT)
            if d > 0:

                @pl.when(first_of_chain(d))
                def _():
                    snd_k[d, g] = part_k[d, g].astype(BF)
                    dk_copy(d, g).start()

            dq[g] += dot(k_t[d, g], ds, NN)

    for d in range(reach, 0, -1):
        pl.when(i >= d)(functools.partial(block, d))
    def relay(d):
        @pl.when(has_up & (i >= d))
        def _():
            for g in range(kv_heads):
                dv_copy(d + 1, g).wait_recv()
                snd_v[d, g] = (part_v[d, g] + rcv_v[d, g].astype(F32)).astype(BF)
                dv_copy(d, g).start()
            for g in range(kv_heads):
                dk_copy(d + 1, g).wait_recv()
                snd_k[d, g] = (part_k[d, g] + rcv_k[d, g].astype(F32)).astype(BF)
                dk_copy(d, g).start()

    if reach >= 2:
        relay(reach - 1)
    c_v.wait()
    block(0)

    coupling = jnp.zeros((1, rows), F32)
    low = []
    for g in range(kv_heads):
        for r in range(group):
            cols = slice(r * rows, (r + 1) * rows)
            part = (dq[g, :, cols] * scale).astype(BF)
            low.append(part)
            coupling = coupling + jnp.sum(
                part.astype(F32) * q_t[g, :, cols].astype(F32), axis=0, keepdims=True
            )
    dq_low = jnp.concatenate(low, axis=0)
    owners = (diag, cross, partner, t)

    def piece_rows(n):
        return pl.ds(pl.multiple_of(owners[n] * width, 16), width)

    def query_piece(n):
        pacc[n] = dot(wq[piece_rows(n), :], dq_low, NN)

    c_wq.wait()
    done = 0
    for d in range(reach - 1, 0, -1):

        if d < reach - 1:
            relay(d)
        if done < 4:
            query_piece(done)
            done += 1
    while done < 4:
        query_piece(done)
        done += 1
    c_wk.wait()
    c_wv.wait()
    c_xin.wait()
    c_inv.wait()
    if reach >= 1:

        @pl.when(has_up)
        def _():
            for g in range(kv_heads):
                dv_copy(1, g).wait_recv()
                part_v[0, g] += rcv_v[0, g].astype(F32)

    dv_low = jnp.concatenate([part_v[0, g].astype(BF) for g in range(kv_heads)], axis=1)
    for n in range(4):
        pacc[n] += dot(wv[piece_rows(n), :], dv_low, NT)
    if reach >= 1:

        @pl.when(has_up)
        def _():
            for g in range(kv_heads):
                dk_copy(1, g).wait_recv()
                part_k[0, g] += rcv_k[0, g].astype(F32)

    dk_low = jnp.concatenate(
        [(part_k[0, g] * scale).astype(BF) for g in range(kv_heads)], axis=1
    )
    both = dk_low.astype(F32) * kb[0].astype(F32) + dv_low.astype(F32) * vb[0].astype(F32)
    for g in range(kv_heads):
        coupling = coupling + jnp.sum(both[:, head_cols(g)].T, axis=0, keepdims=True)

    def piece(n):
        return pacc[n] + dot(wk[piece_rows(n), :], dk_low, NT)

    lead = COUPLING_ROWS
    wide = jnp.broadcast_to(coupling, (lead, rows))

    send_a = remote(rs_a, rs_ar, rs_s.at[0], rs_rv.at[0], {"tp": partner})
    send_c = remote(rs_c, rs_cr, rs_s.at[1], rs_rv.at[1], {"tp": partner})

    def b_copy(n):
        sl = pl.ds(0, lead + chunk) if n == 0 else pl.ds(lead + n * chunk, chunk)
        return remote(
            rs_b.at[sl], rs_br.at[sl], rs_s.at[2 + n], rs_rv.at[2 + n], {"tp": cross}
        )

    def x_copy(n):
        sl = pl.ds(n * chunk, chunk)
        if pipe_n == 1:
            return pltpu.make_async_copy(res.at[sl], out_h.at[sl], x_s.at[n])
        return remote(res.at[sl], out_h.at[sl], x_s.at[n], x_r.at[n], {"pipe": prev})

    rs_a[lead:, :] = piece(0).astype(BF)
    rs_a[:lead, :] = wide.astype(BF)
    send_a.start()
    pacc[1] = piece(1)
    send_a.wait_recv()
    rs_b[:lead, :] = (wide + rs_ar[:lead, :].astype(F32)).astype(BF)
    for n in range(chunks):
        sl = slice(n * chunk, (n + 1) * chunk)
        sh = slice(lead + n * chunk, lead + (n + 1) * chunk)
        rs_b[sh, :] = (pacc[1, sl] + rs_ar[sh, :].astype(F32)).astype(BF)
        b_copy(n).start()
    rs_c[lead:, :] = piece(2).astype(BF)
    rs_c[:lead, :] = wide.astype(BF)
    send_c.start()
    pacc[3] = piece(3)
    iv = inv[...]
    send_c.wait_recv()
    for n in range(chunks):
        sl = slice(n * chunk, (n + 1) * chunk)
        sh = slice(lead + n * chunk, lead + (n + 1) * chunk)
        b_copy(n).wait_recv()
        if n == 0:
            coup = (
                coupling + rs_cr[:lead, :].astype(F32)[:1] + rs_br[:lead, :].astype(F32)[:1]
            )
            drag = iv * coup / model_width
        normed = pacc[3, sl] + rs_cr[sh, :].astype(F32) + rs_br[sh, :].astype(F32)
        val = gath[t, sl, :].astype(F32) + iv * (
            gain_col[sl, :] * normed - xin[sl, :].astype(F32) * drag
        )
        res[sl, :] = val.astype(BF)
        x_copy(n).start()

    for n in range(GATHER_PARTS):
        ag_cross(n).wait_send()
        ag_fwd(n).wait_send()
    ag_part.wait_send()
    for d in range(reach):

        @pl.when(has_up & (i >= d))
        def _():
            k_copy(d).wait_send()
            v_copy(d).wait_send()

    for d in range(1, reach + 1):

        @pl.when(i >= d)
        def _():
            for g in range(kv_heads):
                dv_copy(d, g).wait_send()
                dk_copy(d, g).wait_send()

    send_a.wait_send()
    send_c.wait_send()
    for n in range(chunks):
        b_copy(n).wait_send()
    for n in range(chunks):
        x_copy(n).wait()


def per_device(up, xin, inv, gain, q, k, v, ao, wq, wk, wv, wo, lens):
    ctx_n = lax.axis_size("ctx")
    pipe_n = lax.axis_size("pipe")
    tp_n = lax.axis_size("tp")
    assert tp_n == 4
    up, xin, q, k, v, ao = up[0].T, xin[0].T, q[0], k[0], v[0], ao[0]
    wq, wk, wv, wo = wq[0], wk[0], wv[0], wo[0]
    width, rows = up.shape
    reach = min((WINDOW - 2 + rows) // rows, ctx_n - 1)
    kv_cols, q_cols = k.shape[1], q.shape[1]
    kv_heads = kv_cols // HEAD_SIZE
    stacked = rows * (q_cols // kv_cols)
    chunks = chunk_count(width)
    vm = pltpu.VMEM
    dma = pltpu.SemaphoreType.DMA
    blocks = reach + 1
    scratch = [
        vm((tp_n, width, rows), BF),
        vm((width, rows), BF),
        vm(inv.shape, F32),
        vm(gain.shape, F32),
        vm(q.shape, BF),
        vm((blocks, rows, kv_cols), BF),
        vm((blocks, rows, kv_cols), BF),
        vm(ao.shape, BF),
        vm(wq.shape, BF),
        vm(wk.shape, BF),
        vm(wv.shape, BF),
        vm(wo.shape, BF),
        pltpu.SMEM(lens.shape, jnp.int32),
        vm((tp_n, wo.shape[0], width), BF),
        vm((width, rows), F32),
        vm((q_cols, rows), F32),
        vm((kv_heads, HEAD_SIZE, stacked), BF),
        vm((blocks, kv_heads, HEAD_SIZE, rows), BF),
        vm((kv_heads, HEAD_SIZE, stacked), BF),
        vm((blocks, kv_heads, rows, stacked), F32),
        vm((blocks, kv_heads, rows, HEAD_SIZE), F32),
        vm((blocks, kv_heads, rows, HEAD_SIZE), F32),
        vm((blocks, kv_heads, rows, HEAD_SIZE), BF),
        vm((blocks, kv_heads, rows, HEAD_SIZE), BF),
        vm((blocks, kv_heads, rows, HEAD_SIZE), BF),
        vm((blocks, kv_heads, rows, HEAD_SIZE), BF),
        vm((kv_heads, HEAD_SIZE, stacked), F32),
        vm((tp_n, width, rows), F32),
    ]
    scratch += [vm((COUPLING_ROWS + width, rows), BF)] * 6
    scratch += [vm((width, rows), BF)]
    scratch += [dma((13,))]
    scratch += [dma((blocks,))] * 4
    scratch += [dma((2 * GATHER_PARTS + 1,))] * 2
    scratch += [dma((blocks, kv_heads))] * 4
    scratch += [dma((2 + chunks,))] * 2
    scratch += [dma((chunks,))] * 2
    out = pl.pallas_call(
        functools.partial(kernel, ctx_n, pipe_n, reach),
        out_shape=jax.ShapeDtypeStruct((width, rows), BF),
        in_specs=[pl.BlockSpec(memory_space=pl.ANY)] * 13,
        out_specs=pl.BlockSpec(memory_space=pl.ANY),
        scratch_shapes=scratch,
        compiler_params=pltpu.CompilerParams(collective_id=0, has_side_effects=True),
        name="layer_backward",
    )(up, xin, inv, gain, q, k, v, ao, wq, wk, wv, wo, lens)
    return out.T[None]


def solution(mesh):
    placed = (
        P("pipe", "ctx", "tp"),
        P("pipe", "ctx", "tp"),
        P("pipe", "ctx"),
        P("pipe", "tp"),
        P("pipe", "ctx", "tp"),
        P("pipe", "ctx", "tp"),
        P("pipe", "ctx", "tp"),
        P("pipe", "ctx", "tp"),
        P("pipe", None, "tp"),
        P("pipe", None, "tp"),
        P("pipe", None, "tp"),
        P("pipe", "tp", None),
        P("pipe"),
    )
    return jax.shard_map(
        per_device, mesh=mesh, in_specs=placed, out_specs=P("pipe", "ctx", "tp"), check_vma=False
    )
```
